32 devices in a mesh: grp: 2 (over y), wide: 4 (over z), freq: 2 (over x), pol: 2 (over core).
Axes of the slice: x: 2, y: 2, z: 4, core: 2. Of those that a mesh axis runs over, the one named last changes fastest.
Arguments:
- visibilities: float32 [2, 4096, 8, 384], P(None, ('grp', 'wide'), 'freq', 'pol'), parts along dimension 1, may hold values from -6 to 6
- beams: bfloat16 [8, 8, 2, 384, 768], P('wide', 'freq', None, 'pol'), may hold values from -0.21875 to 0.21875
- spectra: float32 [8, 5, 768], P('freq'), may hold values from 0.1 to 1
- m_orders: int32 [8], replicated, may hold values from 0 to 1023, as said below
Outputs:
- msdata: float32 [16, 8, 2, 384], P(('grp', 'wide'), 'freq', None, 'pol'), parts along dimension 0
- weighted: float32 [16, 8, 2, 384], P(('grp', 'wide'), 'freq', None, 'pol'), parts along dimension 0
The draws below stay inside these ranges and needn't reach their ends.
There are 2 independent parts, one for each index of `grp`. The reference program is written for one: setup_inputs(seed, part) draws one part's arguments, and reference() takes and returns one part's arrays. A program takes and returns all parts, laid end to end along the dimension named above; an argument that names none is the same for every part. Nothing has to cross between parts.
Inputs may be any that keep to these rules, and one draw needn't show every extreme that they name: `m_orders`: the m-orders are distinct, and 0 and 1023 are always among them.
All inputs are finite; a program needn't handle non-finite values.
Results may differ from the reference program's by a relative error of at most 0.0039.
Values sent between devices are 32-bit elements; how exact they have to be, the bound alone decides.
A program may use at most 64 MiB of HBM per device.

```python
import math
import jax
import jax.numpy as jnp
from jax import lax

TIME = 2048
MODES = 384
DEGREES = 768
BAND = 4
M_TOTAL = 8
FBLOCKS = 8


def draw_m_orders(key, part):
    key_one, key_two = jax.random.split(jax.random.fold_in(key, 11))
    inner = jax.random.permutation(key_one, TIME // 2 - 2)[:M_TOTAL - 2] + 1
    ends = jnp.array([0, TIME // 2 - 1], jnp.int32)
    joined = jnp.concatenate([ends, inner.astype(jnp.int32)])
    return jax.random.permutation(key_two, joined).astype(jnp.int32)


def block_levels(rng, shape, cuts, smallest, high):
    def one(position, parts):
        heights = jax.random.uniform(jax.random.fold_in(jax.random.fold_in(rng, 6), position), (parts,), jnp.float32, smallest / len(cuts), high / len(cuts))
        return jnp.repeat(jnp.exp(heights), shape[position] // parts).reshape((-1,) + (1,) * (len(shape) - position - 1))

    factor_of = one(*cuts[0])
    for cut in cuts[1:]:
        factor_of = factor_of * one(*cut)
    return factor_of


def noise(stream_key, dims, scale, most, pieces=(), kind=jnp.bfloat16):
    values = jax.random.normal(stream_key, dims, jnp.float32) * scale
    if len(pieces) > 0:
        values = block_levels(stream_key, dims, pieces, -0.22, 0.18) * values
    return jnp.clip(values, min=-most, max=most).astype(kind)


def setup_inputs(seed: int = 0, part: int = 0) -> dict:
    key_list = jax.random.split(jax.random.key(seed), 5)
    part_keys = jax.random.split(jax.random.fold_in(key_list[4], part), 5)
    return {
        "visibilities": noise(part_keys[0], (2, TIME, FBLOCKS, MODES), 1.0, 6.0, ((1, 4), (2, 2), (3, 2)), jnp.float32),
        "beams": noise(key_list[1], (M_TOTAL, FBLOCKS, 2, MODES, DEGREES), (2 * MODES) ** -0.5, 0.21875, ((0, 4), (1, 2), (3, 2))),
        "spectra": jnp.clip(jnp.exp(math.log(1.0) - 2.3025851 * jax.random.uniform(key_list[2], (FBLOCKS, BAND + 1, DEGREES), jnp.float32) ** block_levels(key_list[2], (FBLOCKS, BAND + 1, DEGREES), ((0, 2),), -0.2, 0.2)), 0.1, 1.0),
        "m_orders": draw_m_orders(jax.random.fold_in(key_list[4], 71), part),
    }


def fourier_tables(orders, times):
    product = orders[:, None] * times[None, :] % TIME
    angle = product.astype(jnp.float32) * (2.0 * math.pi / TIME)
    factor = 1.0 / math.sqrt(TIME)
    return (jnp.cos(angle) * factor, jnp.sin(angle) * factor)

def reference(visibilities, beams, spectra, m_orders):
    times = jnp.arange(TIME, dtype=jnp.int32)
    cosine, sine_tab = fourier_tables(m_orders.astype(jnp.int32), times)
    data_real = visibilities[0].reshape(TIME, -1)
    data_imag = visibilities[1].reshape(TIME, -1)
    exact_mode = lax.Precision.HIGHEST
    part_real = jnp.dot(cosine, data_real, precision=exact_mode, preferred_element_type=jnp.float32) + jnp.dot(sine_tab, data_imag, precision=exact_mode, preferred_element_type=jnp.float32)
    part_imag = jnp.dot(cosine, data_imag, precision=exact_mode, preferred_element_type=jnp.float32) - jnp.dot(sine_tab, data_real, precision=exact_mode, preferred_element_type=jnp.float32)
    part_real = part_real.reshape(M_TOTAL, FBLOCKS, MODES)
    part_imag = part_imag.reshape(M_TOTAL, FBLOCKS, MODES)
    msdata = jnp.stack([part_real, part_imag], axis=2)

    def per_order(items):
        row_data, beam = items
        rounded = lax.optimization_barrier(row_data.astype(jnp.bfloat16)).astype(jnp.float32)
        beam_full = beam.astype(jnp.float32)
        round_real = rounded[:, 0]
        round_imag = rounded[:, 1]
        stacked = jnp.stack([jnp.stack([round_real, round_imag], 1), jnp.stack([round_imag, -round_real], 1)], 1)
        projected = jnp.einsum('fock,fckl->fol', stacked, beam_full, precision=exact_mode)
        mixed = jnp.zeros(projected.shape, jnp.float32)
        for offset in range(BAND + 1):
            mixed = mixed + spectra[:, offset, None, :] * jnp.roll(projected, -offset, axis=0)
        coupled = lax.optimization_barrier(mixed.astype(jnp.bfloat16)).astype(jnp.float32)
        cop_real = coupled[:, 0]
        cop_imag = coupled[:, 1]
        paired = jnp.stack([jnp.stack([cop_real, -cop_imag], 1), jnp.stack([cop_imag, cop_real], 1)], 1)
        return jnp.einsum('focl,fckl->fok', paired, beam_full, precision=exact_mode)
    weighted = lax.map(per_order, (msdata, beams))
    return (msdata, weighted)
```

```python
import functools
import math

import jax
import jax.numpy as jnp
from jax import lax
from jax.experimental import pallas as pl
from jax.experimental.pallas import tpu as pltpu
from jax.sharding import PartitionSpec as P

TIME = 2048
QUARTER = TIME // 4
BAND = 4
PIECES = 2
MESH = pl.DeviceIdType.MESH
NT = (((1,), (1,)), ((), ()))
NN = (((1,), (0,)), ((), ()))


def cosine(steps):
    near = steps + QUARTER // 2
    quadrant = (near // QUARTER) & 3
    x = ((near & (QUARTER - 1)) - QUARTER // 2).astype(jnp.float32) * (2.0 * math.pi / TIME)
    y = x * x
    cos = 1.0 + y * (-1 / 2 + y * (1 / 24 + y * (-1 / 720 + y * (1 / 40320))))
    sin = x * (1.0 + y * (-1 / 6 + y * (1 / 120 + y * (-1 / 5040 + y * (1 / 362880)))))
    value = jnp.where((quadrant & 1) == 1, sin, cos)
    return jnp.where((quadrant == 1) | (quadrant == 2), -value, value)


def high_low(array):
    high = array.astype(jnp.bfloat16)
    return high, (array - high.astype(jnp.float32)).astype(jnp.bfloat16)


def turned(array, sign):
    rows = []
    for order in range(array.shape[0] // 2):
        real, imag = array[2 * order : 2 * order + 1], array[2 * order + 1 : 2 * order + 2]
        rows += [imag, -real] if sign > 0 else [-imag, real]
    return jnp.concatenate(rows, axis=0)


def kernel(
    wide, freq, orders_hbm, vis_hbm, beams_hbm, spectra_hbm, ms_ref, out_ref,
    orders, vis, beams, spectra, part, recv, proj, recv_proj,
    order_sem, vis_sem, beam_sem, spectra_sem, send_sem, recv_sem, psend_sem, precv_sem,
):
    my_wide, my_freq, my_pol = lax.axis_index("wide"), lax.axis_index("freq"), lax.axis_index("pol")
    _, blocks, modes, times = vis.shape
    total, local = orders.shape[0], ms_ref.shape[0]
    rows = 2 * local

    order_copy = pltpu.make_async_copy(orders_hbm, orders, order_sem)
    order_copy.start()
    vis_copies = [
        pltpu.make_async_copy(vis_hbm.at[:, f], vis.at[:, f], vis_sem.at[f]) for f in range(blocks)
    ]
    for copy in vis_copies:
        copy.start()
    before = lax.rem(my_freq + freq - 1, freq)
    after = lax.rem(my_freq + 1, freq)
    barrier = pltpu.get_barrier_semaphore()
    greeted = [{"wide": lax.rem(my_wide + j, wide)} for j in range(1, wide)]
    greeted += [{"pol": 1 - my_pol}, {"freq": before}, {"freq": before, "pol": 1 - my_pol}]
    if freq > 2:
        greeted += [{"freq": after}, {"freq": after, "pol": 1 - my_pol}]
    for device in greeted:
        pl.semaphore_signal(barrier, inc=1, device_id=device, device_id_type=MESH)
    beam_copies = [
        pltpu.make_async_copy(beams_hbm.at[:, f], beams.at[:, f], beam_sem.at[f])
        for f in range(blocks)
    ]
    for copy in beam_copies:
        copy.start()
    spectra_copy = pltpu.make_async_copy(spectra_hbm, spectra, spectra_sem)
    spectra_copy.start()

    shape = (2 * total, times)
    row = lax.broadcasted_iota(jnp.int32, shape, 0)
    time = lax.broadcasted_iota(jnp.int32, shape, 1) + my_wide * times
    order_copy.wait()
    order = jnp.zeros(shape, jnp.int32)
    for i in range(total):
        order = jnp.where(row // 2 == i, orders[i], order)
    steps = order * time
    imag_row = (row & 1) == 1
    factor = 1.0 / math.sqrt(TIME)
    stacks, highs = [], []
    for shift in (jnp.where(imag_row, QUARTER, 0), jnp.where(imag_row, 0, 3 * QUARTER)):
        high, low = high_low(cosine(steps + shift) * factor)
        stacks.append(jnp.concatenate([high, low], axis=0))
        highs.append(high)

    for f in range(blocks):
        vis_copies[f].wait()
        both = jnp.zeros((4 * total, modes), jnp.float32)
        small = jnp.zeros((2 * total, modes), jnp.float32)
        for c in range(2):
            high, low = high_low(vis[c, f])
            both += lax.dot_general(stacks[c], high, NT, preferred_element_type=jnp.float32)
            small += lax.dot_general(highs[c], low, NT, preferred_element_type=jnp.float32)
        result = both[: 2 * total] + (both[2 * total :] + small)
        for w in range(wide):
            part[w, f] = result[rows * w : rows * (w + 1)]

    pl.semaphore_wait(barrier, len(greeted))
    sends = []
    for j in range(1, wide):
        target = lax.rem(my_wide + j, wide)
        copy = pltpu.make_async_remote_copy(
            src_ref=part.at[target],
            dst_ref=recv.at[j - 1],
            send_sem=send_sem.at[j - 1],
            recv_sem=recv_sem.at[j - 1],
            device_id={"wide": target},
            device_id_type=MESH,
        )
        copy.start()
        sends.append(copy)
    for copy in sends:
        copy.wait_recv()

    order_of_row = lax.broadcasted_iota(jnp.int32, (rows, modes), 0) // 2
    targets = [{"pol": 1 - my_pol}, {"freq": before}, {"freq": before, "pol": 1 - my_pol}]
    piece = blocks // PIECES
    proj_sends = []
    for f in range(blocks):
        summed = part[my_wide, f]
        for j in range(wide - 1):
            summed += recv[j, f]
        for o in range(local):
            ms_ref[o, f] = summed[2 * o : 2 * o + 2]
        other = turned(summed, 1)
        beam_copies[f].wait()
        acc = jnp.zeros((rows, beams.shape[-1]), jnp.float32)
        for o in range(local):
            mine = order_of_row == o
            for c, data in ((0, summed), (1, other)):
                left = jnp.where(mine, data, 0.0).astype(jnp.bfloat16)
                acc += lax.dot_general(
                    left, beams[o, f, c], NN, preferred_element_type=jnp.float32
                )
        proj[f] = acc
        if f % piece == piece - 1:
            g = f // piece
            span = pl.ds(g * piece, piece)
            for s, target in enumerate(targets):
                copy = pltpu.make_async_remote_copy(
                    src_ref=proj.at[span],
                    dst_ref=recv_proj.at[s, span],
                    send_sem=psend_sem.at[s, g],
                    recv_sem=precv_sem.at[s, g],
                    device_id=target,
                    device_id_type=MESH,
                )
                copy.start()
                proj_sends.append(copy)
    spectra_copy.wait()
    for copy in proj_sends:
        copy.wait_recv()

    extended = [proj[f] + recv_proj[0, f] for f in range(blocks)]
    extended += [recv_proj[1, f] + recv_proj[2, f] for f in range(blocks)]
    order_of_row = lax.broadcasted_iota(jnp.int32, (rows, beams.shape[-1]), 0) // 2
    for f in range(blocks):
        mixed = spectra[0, f : f + 1] * extended[f]
        for d in range(1, BAND + 1):
            mixed = mixed + spectra[d, f : f + 1] * extended[f + d]
        other = turned(mixed, -1)
        acc = jnp.zeros((rows, modes), jnp.float32)
        for o in range(local):
            mine = order_of_row == o
            for c, data in ((0, mixed), (1, other)):
                left = jnp.where(mine, data, 0.0).astype(jnp.bfloat16)
                acc += lax.dot_general(
                    left, beams[o, f, c], NT, preferred_element_type=jnp.float32
                )
        for o in range(local):
            out_ref[o, f] = acc[2 * o : 2 * o + 2]
    for copy in sends + proj_sends:
        copy.wait_send()


def shards(wide, freq, visibilities, beams, spectra, m_orders):
    local, blocks, _, modes, degrees = beams.shape
    times = visibilities.shape[1]
    rows = 2 * local
    result = jax.ShapeDtypeStruct((local, blocks, 2, modes), jnp.float32)
    dma = pltpu.SemaphoreType.DMA
    return pl.pallas_call(
        functools.partial(kernel, wide, freq),
        out_shape=(result, result),
        in_specs=[pl.BlockSpec(memory_space=pl.ANY)] * 4,
        out_specs=(pl.BlockSpec(memory_space=pltpu.VMEM),) * 2,
        scratch_shapes=[
            pltpu.SMEM(m_orders.shape, jnp.int32),
            pltpu.VMEM((2, blocks, modes, times), jnp.float32),
            pltpu.VMEM(beams.shape, beams.dtype),
            pltpu.VMEM((BAND + 1, blocks, degrees), jnp.float32),
            pltpu.VMEM((wide, blocks, rows, modes), jnp.float32),
            pltpu.VMEM((wide - 1, blocks, rows, modes), jnp.float32),
            pltpu.VMEM((blocks, rows, degrees), jnp.float32),
            pltpu.VMEM((3, blocks, rows, degrees), jnp.float32),
            dma,
            dma((blocks,)),
            dma((blocks,)),
            dma,
            dma((wide - 1,)),
            dma((wide - 1,)),
            dma((3, PIECES)),
            dma((3, PIECES)),
        ],
        compiler_params=pltpu.CompilerParams(
            collective_id=0, has_side_effects=True, vmem_limit_bytes=48 << 20
        ),
    )(
        m_orders,
        jnp.transpose(visibilities, (0, 2, 3, 1)),
        beams,
        jnp.transpose(spectra, (1, 0, 2)),
    )


def solution(mesh):
    return jax.shard_map(
        functools.partial(shards, mesh.shape["wide"], mesh.shape["freq"]),
        mesh=mesh,
        in_specs=(
            P(None, ("grp", "wide"), "freq", "pol"),
            P("wide", "freq", None, "pol", None),
            P("freq", None, None),
            P(),
        ),
        out_specs=(
            P(("grp", "wide"), "freq", None, "pol"),
            P(("grp", "wide"), "freq", None, "pol"),
        ),
        check_vma=False,
    )
```

```python
import functools
import math

import jax
import jax.numpy as jnp
from jax import lax
from jax.experimental import pallas as pl
from jax.experimental.pallas import tpu as pltpu
from jax.sharding import PartitionSpec as P

TIME = 2048
QUARTER = TIME // 4
BAND = 4
PIECES = 2
MESH = pl.DeviceIdType.MESH
NT = (((1,), (1,)), ((), ()))
NN = (((1,), (0,)), ((), ()))


def cosine(steps):
    near = steps + QUARTER // 2
    quadrant = (near // QUARTER) & 3
    x = ((near & (QUARTER - 1)) - QUARTER // 2).astype(jnp.float32) * (2.0 * math.pi / TIME)
    y = x * x
    cos = 1.0 + y * (-1 / 2 + y * (1 / 24 + y * (-1 / 720 + y * (1 / 40320))))
    sin = x * (1.0 + y * (-1 / 6 + y * (1 / 120 + y * (-1 / 5040 + y * (1 / 362880)))))
    value = jnp.where((quadrant & 1) == 1, sin, cos)
    return jnp.where((quadrant == 1) | (quadrant == 2), -value, value)


def high_low(array):
    high = array.astype(jnp.bfloat16)
    return high, (array - high.astype(jnp.float32)).astype(jnp.bfloat16)


def turned(array, sign):
    rows = []
    for order in range(array.shape[0] // 2):
        real, imag = array[2 * order : 2 * order + 1], array[2 * order + 1 : 2 * order + 2]
        rows += [imag, -real] if sign > 0 else [-imag, real]
    return jnp.concatenate(rows, axis=0)


def kernel(
    wide, freq, orders_hbm, vis_hbm, beams_hbm, spectra_hbm, result_ref,
    orders, vis, beams, spectra, part, recv, proj, recv_proj,
    order_sem, vis_sem, beam_sem, spectra_sem, send_sem, recv_sem, psend_sem, precv_sem,
):
    my_wide, my_freq, my_pol = lax.axis_index("wide"), lax.axis_index("freq"), lax.axis_index("pol")
    ms_ref, out_ref = result_ref.at[0], result_ref.at[1]
    _, blocks, modes, times = vis.shape
    total, local = orders.shape[0], ms_ref.shape[0]
    rows = 2 * local

    order_copy = pltpu.make_async_copy(orders_hbm, orders, order_sem)
    order_copy.start()
    vis_copies = [
        pltpu.make_async_copy(vis_hbm.at[:, f], vis.at[:, f], vis_sem.at[f]) for f in range(blocks)
    ]
    for copy in vis_copies:
        copy.start()
    before = lax.rem(my_freq + freq - 1, freq)
    after = lax.rem(my_freq + 1, freq)
    barrier = pltpu.get_barrier_semaphore()
    greeted = [{"wide": lax.rem(my_wide + j, wide)} for j in range(1, wide)]
    greeted += [{"pol": 1 - my_pol}, {"freq": before}, {"freq": before, "pol": 1 - my_pol}]
    if freq > 2:
        greeted += [{"freq": after}, {"freq": after, "pol": 1 - my_pol}]
    for device in greeted:
        pl.semaphore_signal(barrier, inc=1, device_id=device, device_id_type=MESH)
    beam_copies = [
        pltpu.make_async_copy(beams_hbm.at[:, f], beams.at[:, f], beam_sem.at[f])
        for f in range(blocks)
    ]
    for copy in beam_copies:
        copy.start()
    spectra_copy = pltpu.make_async_copy(spectra_hbm, spectra, spectra_sem)
    spectra_copy.start()

    shape = (2 * total, times)
    row = lax.broadcasted_iota(jnp.int32, shape, 0)
    time = lax.broadcasted_iota(jnp.int32, shape, 1) + my_wide * times
    order_copy.wait()
    order = jnp.zeros(shape, jnp.int32)
    for i in range(total):
        order = jnp.where(row // 2 == i, orders[i], order)
    steps = order * time
    imag_row = (row & 1) == 1
    factor = 1.0 / math.sqrt(TIME)
    stacks, highs = [], []
    for shift in (jnp.where(imag_row, QUARTER, 0), jnp.where(imag_row, 0, 3 * QUARTER)):
        high, low = high_low(cosine(steps + shift) * factor)
        stacks.append(jnp.concatenate([high, low], axis=0))
        highs.append(high)

    for f in range(blocks):
        vis_copies[f].wait()
        both = jnp.zeros((4 * total, modes), jnp.float32)
        small = jnp.zeros((2 * total, modes), jnp.float32)
        for c in range(2):
            high, low = high_low(vis[c, f])
            both += lax.dot_general(stacks[c], high, NT, preferred_element_type=jnp.float32)
            small += lax.dot_general(highs[c], low, NT, preferred_element_type=jnp.float32)
        result = both[: 2 * total] + (both[2 * total :] + small)
        for w in range(wide):
            part[w, f] = result[rows * w : rows * (w + 1)]

    pl.semaphore_wait(barrier, len(greeted))
    sends = []
    for j in range(1, wide):
        target = lax.rem(my_wide + j, wide)
        copy = pltpu.make_async_remote_copy(
            src_ref=part.at[target],
            dst_ref=recv.at[j - 1],
            send_sem=send_sem.at[j - 1],
            recv_sem=recv_sem.at[j - 1],
            device_id={"wide": target},
            device_id_type=MESH,
        )
        copy.start()
        sends.append(copy)
    for copy in sends:
        copy.wait_recv()

    order_of_row = lax.broadcasted_iota(jnp.int32, (rows, modes), 0) // 2
    targets = [{"pol": 1 - my_pol}, {"freq": before}, {"freq": before, "pol": 1 - my_pol}]
    piece = blocks // PIECES
    proj_sends = []
    for f in range(blocks):
        summed = part[my_wide, f]
        for j in range(wide - 1):
            summed += recv[j, f]
        for o in range(local):
            ms_ref[o, f] = summed[2 * o : 2 * o + 2]
        other = turned(summed, 1)
        beam_copies[f].wait()
        acc = jnp.zeros((rows, beams.shape[-1]), jnp.float32)
        for o in range(local):
            mine = order_of_row == o
            for c, data in ((0, summed), (1, other)):
                left = jnp.where(mine, data, 0.0).astype(jnp.bfloat16)
                acc += lax.dot_general(
                    left, beams[o, f, c], NN, preferred_element_type=jnp.float32
                )
        proj[f] = acc
        if f % piece == piece - 1:
            g = f // piece
            span = pl.ds(g * piece, piece)
            for s, target in enumerate(targets):
                copy = pltpu.make_async_remote_copy(
                    src_ref=proj.at[span],
                    dst_ref=recv_proj.at[s, span],
                    send_sem=psend_sem.at[s, g],
                    recv_sem=precv_sem.at[s, g],
                    device_id=target,
                    device_id_type=MESH,
                )
                copy.start()
                proj_sends.append(copy)
    spectra_copy.wait()
    for copy in proj_sends:
        copy.wait_recv()

    extended = [proj[f] + recv_proj[0, f] for f in range(blocks)]
    extended += [recv_proj[1, f] + recv_proj[2, f] for f in range(blocks)]
    order_of_row = lax.broadcasted_iota(jnp.int32, (rows, beams.shape[-1]), 0) // 2
    for f in range(blocks):
        mixed = spectra[0, f : f + 1] * extended[f]
        for d in range(1, BAND + 1):
            mixed = mixed + spectra[d, f : f + 1] * extended[f + d]
        other = turned(mixed, -1)
        acc = jnp.zeros((rows, modes), jnp.float32)
        for o in range(local):
            mine = order_of_row == o
            for c, data in ((0, mixed), (1, other)):
                left = jnp.where(mine, data, 0.0).astype(jnp.bfloat16)
                acc += lax.dot_general(
                    left, beams[o, f, c], NT, preferred_element_type=jnp.float32
                )
        for o in range(local):
            out_ref[o, f] = acc[2 * o : 2 * o + 2]
    for copy in sends + proj_sends:
        copy.wait_send()


def shards(wide, freq, visibilities, beams, spectra, m_orders):
    local, blocks, _, modes, degrees = beams.shape
    times = visibilities.shape[1]
    rows = 2 * local
    result = jax.ShapeDtypeStruct((2, local, blocks, 2, modes), jnp.float32)
    dma = pltpu.SemaphoreType.DMA
    both = pl.pallas_call(
        functools.partial(kernel, wide, freq),
        out_shape=result,
        in_specs=[pl.BlockSpec(memory_space=pl.ANY)] * 4,
        out_specs=pl.BlockSpec(memory_space=pltpu.VMEM),
        scratch_shapes=[
            pltpu.SMEM(m_orders.shape, jnp.int32),
            pltpu.VMEM((2, blocks, modes, times), jnp.float32),
            pltpu.VMEM(beams.shape, beams.dtype),
            pltpu.VMEM((BAND + 1, blocks, degrees), jnp.float32),
            pltpu.VMEM((wide, blocks, rows, modes), jnp.float32),
            pltpu.VMEM((wide - 1, blocks, rows, modes), jnp.float32),
            pltpu.VMEM((blocks, rows, degrees), jnp.float32),
            pltpu.VMEM((3, blocks, rows, degrees), jnp.float32),
            dma,
            dma((blocks,)),
            dma((blocks,)),
            dma,
            dma((wide - 1,)),
            dma((wide - 1,)),
            dma((3, PIECES)),
            dma((3, PIECES)),
        ],
        compiler_params=pltpu.CompilerParams(
            collective_id=0, has_side_effects=True, vmem_limit_bytes=64 << 20
        ),
    )(
        m_orders,
        jnp.transpose(visibilities, (0, 2, 3, 1)),
        beams,
        jnp.transpose(spectra, (1, 0, 2)),
    )
    return both[0], both[1]


def solution(mesh):
    return jax.shard_map(
        functools.partial(shards, mesh.shape["wide"], mesh.shape["freq"]),
        mesh=mesh,
        in_specs=(
            P(None, ("grp", "wide"), "freq", "pol"),
            P("wide", "freq", None, "pol", None),
            P("freq", None, None),
            P(),
        ),
        out_specs=(
            P(("grp", "wide"), "freq", None, "pol"),
            P(("grp", "wide"), "freq", None, "pol"),
        ),
        check_vma=False,
    )
```

```python
import functools
import math

import jax
import jax.numpy as jnp
from jax import lax
from jax.experimental import pallas as pl
from jax.experimental.pallas import tpu as pltpu
from jax.sharding import PartitionSpec as P

TIME = 2048
QUARTER = TIME // 4
SHIFT = QUARTER.bit_length() - 1
BAND = 4
MESH = pl.DeviceIdType.MESH
NT = (((1,), (1,)), ((), ()))
NN = (((1,), (0,)), ((), ()))


def cosine(steps):
    near = steps + QUARTER // 2
    quadrant = (near >> SHIFT) & 3
    x = ((near & (QUARTER - 1)) - QUARTER // 2).astype(jnp.float32) * (2.0 * math.pi / TIME)
    y = x * x
    cos = 1.0 + y * (-1 / 2 + y * (1 / 24 + y * (-1 / 720 + y * (1 / 40320))))
    sin = x * (1.0 + y * (-1 / 6 + y * (1 / 120 + y * (-1 / 5040 + y * (1 / 362880)))))
    value = jnp.where((quadrant & 1) == 1, sin, cos)
    return jnp.where((quadrant == 1) | (quadrant == 2), -value, value)


def high_low(array):
    high = array.astype(jnp.bfloat16)
    return high, (array - high.astype(jnp.float32)).astype(jnp.bfloat16)


def turned(array, sign):
    rows = []
    for order in range(array.shape[0] // 2):
        real, imag = array[2 * order : 2 * order + 1], array[2 * order + 1 : 2 * order + 2]
        rows += [imag, -real] if sign > 0 else [-imag, real]
    return jnp.concatenate(rows, axis=0)


def kernel(
    wide, freq, orders_hbm, vis_hbm, beams_hbm, spectra_hbm, result_ref,
    orders, vis, beams, spectra, part, recv, proj, recv_proj,
    order_sem, vis_sem, beam_sem, spectra_sem, send_sem, recv_sem, psend_sem, precv_sem,
):
    my_wide, my_freq, my_pol = lax.axis_index("wide"), lax.axis_index("freq"), lax.axis_index("pol")
    ms_ref, out_ref = result_ref.at[0], result_ref.at[1]
    _, blocks, modes, times = vis.shape
    total, local = orders.shape[0], ms_ref.shape[0]
    rows = 2 * local

    order_copy = pltpu.make_async_copy(orders_hbm, orders, order_sem)
    order_copy.start()
    vis_copies = [
        pltpu.make_async_copy(vis_hbm.at[:, f], vis.at[:, f], vis_sem.at[f]) for f in range(blocks)
    ]
    for copy in vis_copies:
        copy.start()
    before = lax.rem(my_freq + freq - 1, freq)
    after = lax.rem(my_freq + 1, freq)
    barrier = pltpu.get_barrier_semaphore()
    greeted = [{"wide": lax.rem(my_wide + j, wide)} for j in range(1, wide)]
    greeted += [{"pol": 1 - my_pol}, {"freq": before}, {"freq": before, "pol": 1 - my_pol}]
    if freq > 2:
        greeted += [{"freq": after}, {"freq": after, "pol": 1 - my_pol}]
    for device in greeted:
        pl.semaphore_signal(barrier, inc=1, device_id=device, device_id_type=MESH)
    beam_copies = [
        pltpu.make_async_copy(beams_hbm.at[:, f], beams.at[:, f], beam_sem.at[f])
        for f in range(blocks)
    ]
    for copy in beam_copies:
        copy.start()
    spectra_copy = pltpu.make_async_copy(spectra_hbm, spectra, spectra_sem)
    spectra_copy.start()

    shape = (2 * total, times)
    row = lax.broadcasted_iota(jnp.int32, shape, 0)
    time = lax.broadcasted_iota(jnp.int32, shape, 1) + my_wide * times
    order_copy.wait()
    order = jnp.zeros(shape, jnp.int32)
    for i in range(total):
        order = jnp.where(row >> 1 == i, orders[i], order)
    steps = order * time
    imag_row = (row & 1) == 1
    factor = 1.0 / math.sqrt(TIME)
    stacks, highs = [], []
    for shift in (jnp.where(imag_row, QUARTER, 0), jnp.where(imag_row, 0, 3 * QUARTER)):
        high, low = high_low(cosine(steps + shift) * factor)
        stacks.append(jnp.concatenate([high, low], axis=0))
        highs.append(high)

    for f in range(blocks):
        vis_copies[f].wait()
        both = jnp.zeros((4 * total, modes), jnp.float32)
        small = jnp.zeros((2 * total, modes), jnp.float32)
        for c in range(2):
            high, low = high_low(vis[c, f])
            both += lax.dot_general(stacks[c], high, NT, preferred_element_type=jnp.float32)
            small += lax.dot_general(highs[c], low, NT, preferred_element_type=jnp.float32)
        result = both[: 2 * total] + (both[2 * total :] + small)
        for w in range(wide):
            part[w, f] = result[rows * w : rows * (w + 1)]

    pl.semaphore_wait(barrier, len(greeted))
    sends = []
    for j in range(1, wide):
        target = lax.rem(my_wide + j, wide)
        copy = pltpu.make_async_remote_copy(
            src_ref=part.at[target],
            dst_ref=recv.at[j - 1],
            send_sem=send_sem.at[j - 1],
            recv_sem=recv_sem.at[j - 1],
            device_id={"wide": target},
            device_id_type=MESH,
        )
        copy.start()
        sends.append(copy)
    for copy in sends:
        copy.wait_recv()

    order_of_row = lax.broadcasted_iota(jnp.int32, (rows, modes), 0) >> 1
    targets = [{"pol": 1 - my_pol}, {"freq": before}, {"freq": before, "pol": 1 - my_pol}]
    proj_sends = []
    for f in range(blocks):
        summed = part[my_wide, f]
        for j in range(wide - 1):
            summed += recv[j, f]
        for o in range(local):
            ms_ref[o, f] = summed[2 * o : 2 * o + 2]
        other = turned(summed, 1)
        beam_copies[f].wait()
        acc = jnp.zeros((rows, beams.shape[-1]), jnp.float32)
        for o in range(local):
            mine = order_of_row == o
            for c, data in ((0, summed), (1, other)):
                left = jnp.where(mine, data, 0.0).astype(jnp.bfloat16)
                acc += lax.dot_general(
                    left, beams[o, f, c], NN, preferred_element_type=jnp.float32
                )
        proj[f] = acc
        for s, target in enumerate(targets):
            copy = pltpu.make_async_remote_copy(
                src_ref=proj.at[f],
                dst_ref=recv_proj.at[s, f],
                send_sem=psend_sem.at[s, f],
                recv_sem=precv_sem.at[s, f],
                device_id=target,
                device_id_type=MESH,
            )
            copy.start()
            proj_sends.append(copy)
    spectra_copy.wait()
    for copy in proj_sends:
        copy.wait_recv()

    extended = [proj[f] + recv_proj[0, f] for f in range(blocks)]
    extended += [recv_proj[1, f] + recv_proj[2, f] for f in range(blocks)]
    order_of_row = lax.broadcasted_iota(jnp.int32, (rows, beams.shape[-1]), 0) >> 1
    for f in range(blocks):
        mixed = spectra[0, f : f + 1] * extended[f]
        for d in range(1, BAND + 1):
            mixed = mixed + spectra[d, f : f + 1] * extended[f + d]
        other = turned(mixed, -1)
        acc = jnp.zeros((rows, modes), jnp.float32)
        for o in range(local):
            mine = order_of_row == o
            for c, data in ((0, mixed), (1, other)):
                left = jnp.where(mine, data, 0.0).astype(jnp.bfloat16)
                acc += lax.dot_general(
                    left, beams[o, f, c], NT, preferred_element_type=jnp.float32
                )
        for o in range(local):
            out_ref[o, f] = acc[2 * o : 2 * o + 2]
    for copy in sends + proj_sends:
        copy.wait_send()


def shards(wide, freq, visibilities, beams, spectra, m_orders):
    local, blocks, _, modes, degrees = beams.shape
    times = visibilities.shape[1]
    rows = 2 * local
    result = jax.ShapeDtypeStruct((2, local, blocks, 2, modes), jnp.float32)
    dma = pltpu.SemaphoreType.DMA
    both = pl.pallas_call(
        functools.partial(kernel, wide, freq),
        out_shape=result,
        in_specs=[pl.BlockSpec(memory_space=pl.ANY)] * 4,
        out_specs=pl.BlockSpec(memory_space=pltpu.VMEM),
        scratch_shapes=[
            pltpu.SMEM(m_orders.shape, jnp.int32),
            pltpu.VMEM((2, blocks, modes, times), jnp.float32),
            pltpu.VMEM(beams.shape, beams.dtype),
            pltpu.VMEM((BAND + 1, blocks, degrees), jnp.float32),
            pltpu.VMEM((wide, blocks, rows, modes), jnp.float32),
            pltpu.VMEM((wide - 1, blocks, rows, modes), jnp.float32),
            pltpu.VMEM((blocks, rows, degrees), jnp.float32),
            pltpu.VMEM((3, blocks, rows, degrees), jnp.float32),
            dma,
            dma((blocks,)),
            dma((blocks,)),
            dma,
            dma((wide - 1,)),
            dma((wide - 1,)),
            dma((3, blocks)),
            dma((3, blocks)),
        ],
        compiler_params=pltpu.CompilerParams(
            collective_id=0, has_side_effects=True, vmem_limit_bytes=48 << 20
        ),
    )(
        *(
            pltpu.with_memory_space_constraint(array, pltpu.HBM)
            for array in (
                m_orders,
                jnp.transpose(visibilities, (0, 2, 3, 1)),
                beams,
                jnp.transpose(spectra, (1, 0, 2)),
            )
        )
    )
    return both[0], both[1]


def solution(mesh):
    return jax.shard_map(
        functools.partial(shards, mesh.shape["wide"], mesh.shape["freq"]),
        mesh=mesh,
        in_specs=(
            P(None, ("grp", "wide"), "freq", "pol"),
            P("wide", "freq", None, "pol", None),
            P("freq", None, None),
            P(),
        ),
        out_specs=(
            P(("grp", "wide"), "freq", None, "pol"),
            P(("grp", "wide"), "freq", None, "pol"),
        ),
        check_vma=False,
    )
```

```python
import functools
import math

import jax
import jax.numpy as jnp
from jax import lax
from jax.experimental import pallas as pl
from jax.experimental.pallas import tpu as pltpu
from jax.sharding import PartitionSpec as P

TIME = 2048
QUARTER = TIME // 4
SHIFT = QUARTER.bit_length() - 1
BAND = 4
MESH = pl.DeviceIdType.MESH
NT = (((1,), (1,)), ((), ()))
NN = (((1,), (0,)), ((), ()))


def cosine(steps):
    near = steps + QUARTER // 2
    quadrant = (near >> SHIFT) & 3
    x = ((near & (QUARTER - 1)) - QUARTER // 2).astype(jnp.float32) * (2.0 * math.pi / TIME)
    y = x * x
    cos = 1.0 + y * (-1 / 2 + y * (1 / 24 + y * (-1 / 720 + y * (1 / 40320))))
    sin = x * (1.0 + y * (-1 / 6 + y * (1 / 120 + y * (-1 / 5040 + y * (1 / 362880)))))
    value = jnp.where((quadrant & 1) == 1, sin, cos)
    return jnp.where((quadrant == 1) | (quadrant == 2), -value, value)


def high_low(array):
    high = array.astype(jnp.bfloat16)
    return high, (array - high.astype(jnp.float32)).astype(jnp.bfloat16)


def turned(array, sign):
    rows = []
    for order in range(array.shape[0] // 2):
        real, imag = array[2 * order : 2 * order + 1], array[2 * order + 1 : 2 * order + 2]
        rows += [imag, -real] if sign > 0 else [-imag, real]
    return jnp.concatenate(rows, axis=0)


def kernel(
    wide, freq, orders_hbm, vis_hbm, beams_hbm, spectra_hbm, result_ref,
    orders, vis, beams, spectra, part, recv, proj, recv_proj,
    order_sem, vis_sem, beam_sem, spectra_sem, send_sem, recv_sem, psend_sem, precv_sem,
):
    my_wide, my_freq, my_pol = lax.axis_index("wide"), lax.axis_index("freq"), lax.axis_index("pol")
    ms_ref, out_ref = result_ref.at[0], result_ref.at[1]
    _, blocks, modes, times = vis.shape
    total, local = orders.shape[0], ms_ref.shape[0]
    rows = 2 * local

    order_copy = pltpu.make_async_copy(orders_hbm, orders, order_sem)
    order_copy.start()
    vis_copies = [
        pltpu.make_async_copy(vis_hbm.at[:, f], vis.at[:, f], vis_sem.at[f]) for f in range(blocks)
    ]
    for copy in vis_copies:
        copy.start()
    before = lax.rem(my_freq + freq - 1, freq)
    after = lax.rem(my_freq + 1, freq)
    barrier = pltpu.get_barrier_semaphore()
    greeted = [{"wide": lax.rem(my_wide + j, wide)} for j in range(1, wide)]
    greeted += [{"pol": 1 - my_pol}, {"freq": before}, {"freq": before, "pol": 1 - my_pol}]
    if freq > 2:
        greeted += [{"freq": after}, {"freq": after, "pol": 1 - my_pol}]
    for device in greeted:
        pl.semaphore_signal(barrier, inc=1, device_id=device, device_id_type=MESH)
    beam_copies = [
        pltpu.make_async_copy(beams_hbm.at[:, f], beams.at[:, f], beam_sem.at[f])
        for f in range(blocks)
    ]
    spectra_copy = pltpu.make_async_copy(spectra_hbm, spectra, spectra_sem)
    spectra_copy.start()

    shape = (2 * total, times)
    row = lax.broadcasted_iota(jnp.int32, shape, 0)
    time = lax.broadcasted_iota(jnp.int32, shape, 1) + my_wide * times
    order_copy.wait()
    order = jnp.zeros(shape, jnp.int32)
    for i in range(total):
        order = jnp.where(row >> 1 == i, orders[i], order)
    steps = order * time
    imag_row = (row & 1) == 1
    factor = 1.0 / math.sqrt(TIME)
    stacks, highs = [], []
    for shift in (jnp.where(imag_row, QUARTER, 0), jnp.where(imag_row, 0, 3 * QUARTER)):
        high, low = high_low(cosine(steps + shift) * factor)
        stacks.append(jnp.concatenate([high, low], axis=0))
        highs.append(high)

    for f in range(blocks):
        vis_copies[f].wait()
        if f == blocks - 1:
            for copy in beam_copies:
                copy.start()
        both = jnp.zeros((4 * total, modes), jnp.float32)
        small = jnp.zeros((2 * total, modes), jnp.float32)
        for c in range(2):
            high, low = high_low(vis[c, f])
            both += lax.dot_general(stacks[c], high, NT, preferred_element_type=jnp.float32)
            small += lax.dot_general(highs[c], low, NT, preferred_element_type=jnp.float32)
        result = both[: 2 * total] + (both[2 * total :] + small)
        for w in range(wide):
            part[w, f] = result[rows * w : rows * (w + 1)]

    pl.semaphore_wait(barrier, len(greeted))
    sends = []
    for j in range(1, wide):
        target = lax.rem(my_wide + j, wide)
        copy = pltpu.make_async_remote_copy(
            src_ref=part.at[target],
            dst_ref=recv.at[j - 1],
            send_sem=send_sem.at[j - 1],
            recv_sem=recv_sem.at[j - 1],
            device_id={"wide": target},
            device_id_type=MESH,
        )
        copy.start()
        sends.append(copy)
    for copy in sends:
        copy.wait_recv()

    order_of_row = lax.broadcasted_iota(jnp.int32, (rows, modes), 0) >> 1
    targets = [{"freq": before}, {"freq": before, "pol": 1 - my_pol}, {"pol": 1 - my_pol}]
    proj_sends = []
    for f in range(blocks):
        summed = part[my_wide, f]
        for j in range(wide - 1):
            summed += recv[j, f]
        for o in range(local):
            ms_ref[o, f] = summed[2 * o : 2 * o + 2]
        other = turned(summed, 1)
        beam_copies[f].wait()
        acc = jnp.zeros((rows, beams.shape[-1]), jnp.float32)
        for o in range(local):
            mine = order_of_row == o
            for c, data in ((0, summed), (1, other)):
                left = jnp.where(mine, data, 0.0).astype(jnp.bfloat16)
                acc += lax.dot_general(
                    left, beams[o, f, c], NN, preferred_element_type=jnp.float32
                )
        proj[f] = acc
        for s, target in enumerate(targets):
            copy = pltpu.make_async_remote_copy(
                src_ref=proj.at[f],
                dst_ref=recv_proj.at[s, f],
                send_sem=psend_sem.at[s, f],
                recv_sem=precv_sem.at[s, f],
                device_id=target,
                device_id_type=MESH,
            )
            copy.start()
            proj_sends.append(copy)
    spectra_copy.wait()
    extended = []
    for f in range(blocks):
        proj_sends[3 * f + 2].wait_recv()
        extended.append(proj[f] + recv_proj[2, f])
    order_of_row = lax.broadcasted_iota(jnp.int32, (rows, beams.shape[-1]), 0) >> 1
    for f in range(blocks):
        proj_sends[3 * f].wait_recv()
        proj_sends[3 * f + 1].wait_recv()
        extended.append(recv_proj[0, f] + recv_proj[1, f])
        mixed = spectra[0, f : f + 1] * extended[f]
        for d in range(1, BAND + 1):
            mixed = mixed + spectra[d, f : f + 1] * extended[f + d]
        other = turned(mixed, -1)
        acc = jnp.zeros((rows, modes), jnp.float32)
        for o in range(local):
            mine = order_of_row == o
            for c, data in ((0, mixed), (1, other)):
                left = jnp.where(mine, data, 0.0).astype(jnp.bfloat16)
                acc += lax.dot_general(
                    left, beams[o, f, c], NT, preferred_element_type=jnp.float32
                )
        for o in range(local):
            out_ref[o, f] = acc[2 * o : 2 * o + 2]
    for copy in sends + proj_sends:
        copy.wait_send()


def shards(wide, freq, visibilities, beams, spectra, m_orders):
    local, blocks, _, modes, degrees = beams.shape
    times = visibilities.shape[1]
    rows = 2 * local
    result = jax.ShapeDtypeStruct((2, local, blocks, 2, modes), jnp.float32)
    dma = pltpu.SemaphoreType.DMA
    both = pl.pallas_call(
        functools.partial(kernel, wide, freq),
        out_shape=result,
        in_specs=[pl.BlockSpec(memory_space=pl.ANY)] * 4,
        out_specs=pl.BlockSpec(memory_space=pltpu.VMEM),
        scratch_shapes=[
            pltpu.SMEM(m_orders.shape, jnp.int32),
            pltpu.VMEM((2, blocks, modes, times), jnp.float32),
            pltpu.VMEM(beams.shape, beams.dtype),
            pltpu.VMEM((BAND + 1, blocks, degrees), jnp.float32),
            pltpu.VMEM((wide, blocks, rows, modes), jnp.float32),
            pltpu.VMEM((wide - 1, blocks, rows, modes), jnp.float32),
            pltpu.VMEM((blocks, rows, degrees), jnp.float32),
            pltpu.VMEM((3, blocks, rows, degrees), jnp.float32),
            dma,
            dma((blocks,)),
            dma((blocks,)),
            dma,
            dma((wide - 1,)),
            dma((wide - 1,)),
            dma((3, blocks)),
            dma((3, blocks)),
        ],
        compiler_params=pltpu.CompilerParams(
            collective_id=0, has_side_effects=True, vmem_limit_bytes=48 << 20
        ),
    )(
        *(
            pltpu.with_memory_space_constraint(array, pltpu.HBM)
            for array in (
                m_orders,
                jnp.transpose(visibilities, (0, 2, 3, 1)),
                beams,
                jnp.transpose(spectra, (1, 0, 2)),
            )
        )
    )
    return both[0], both[1]


def solution(mesh):
    return jax.shard_map(
        functools.partial(shards, mesh.shape["wide"], mesh.shape["freq"]),
        mesh=mesh,
        in_specs=(
            P(None, ("grp", "wide"), "freq", "pol"),
            P("wide", "freq", None, "pol", None),
            P("freq", None, None),
            P(),
        ),
        out_specs=(
            P(("grp", "wide"), "freq", None, "pol"),
            P(("grp", "wide"), "freq", None, "pol"),
        ),
        check_vma=False,
    )
```

```python
import functools
import math

import jax
import jax.numpy as jnp
from jax import lax
from jax.experimental import pallas as pl
from jax.experimental.pallas import tpu as pltpu
from jax.sharding import PartitionSpec as P

TIME = 2048
QUARTER = TIME // 4
SHIFT = QUARTER.bit_length() - 1
BAND = 4
MESH = pl.DeviceIdType.MESH
NT = (((1,), (1,)), ((), ()))
NN = (((1,), (0,)), ((), ()))


def cosine(steps):
    near = steps + QUARTER // 2
    quadrant = (near >> SHIFT) & 3
    x = ((near & (QUARTER - 1)) - QUARTER // 2).astype(jnp.float32) * (2.0 * math.pi / TIME)
    y = x * x
    cos = 1.0 + y * (-1 / 2 + y * (1 / 24 + y * (-1 / 720 + y * (1 / 40320))))
    sin = x * (1.0 + y * (-1 / 6 + y * (1 / 120 + y * (-1 / 5040 + y * (1 / 362880)))))
    value = jnp.where((quadrant & 1) == 1, sin, cos)
    return jnp.where((quadrant == 1) | (quadrant == 2), -value, value)


def high_low(array):
    high = array.astype(jnp.bfloat16)
    return high, (array - high.astype(jnp.float32)).astype(jnp.bfloat16)


def turned(array, sign):
    rows = []
    for order in range(array.shape[0] // 2):
        real, imag = array[2 * order : 2 * order + 1], array[2 * order + 1 : 2 * order + 2]
        rows += [imag, -real] if sign > 0 else [-imag, real]
    return jnp.concatenate(rows, axis=0)


def kernel(
    wide, freq, orders_hbm, vis_hbm, beams_hbm, spectra_hbm, result_ref,
    orders, vis, beams, spectra, part, recv, proj, recv_proj,
    order_sem, vis_sem, beam_sem, spectra_sem, send_sem, recv_sem, psend_sem, precv_sem,
):
    my_wide, my_freq, my_pol = lax.axis_index("wide"), lax.axis_index("freq"), lax.axis_index("pol")
    ms_ref, out_ref = result_ref.at[0], result_ref.at[1]
    _, blocks, modes, times = vis.shape
    total, local = orders.shape[0], ms_ref.shape[0]
    rows = 2 * local

    order_copy = pltpu.make_async_copy(orders_hbm, orders, order_sem)
    order_copy.start()
    vis_copies = [
        pltpu.make_async_copy(vis_hbm.at[:, f], vis.at[:, f], vis_sem.at[f]) for f in range(blocks)
    ]
    for copy in vis_copies:
        copy.start()
    before = lax.rem(my_freq + freq - 1, freq)
    after = lax.rem(my_freq + 1, freq)
    barrier = pltpu.get_barrier_semaphore()
    greeted = [{"wide": lax.rem(my_wide + j, wide)} for j in range(1, wide)]
    greeted += [{"pol": 1 - my_pol}, {"freq": before}, {"freq": before, "pol": 1 - my_pol}]
    if freq > 2:
        greeted += [{"freq": after}, {"freq": after, "pol": 1 - my_pol}]
    for device in greeted:
        pl.semaphore_signal(barrier, inc=1, device_id=device, device_id_type=MESH)
    beam_copies = [
        pltpu.make_async_copy(beams_hbm.at[:, f], beams.at[:, f], beam_sem.at[f])
        for f in range(blocks)
    ]
    for copy in beam_copies:
        copy.start()
    spectra_copy = pltpu.make_async_copy(spectra_hbm, spectra, spectra_sem)
    spectra_copy.start()

    shape = (2 * total, times)
    row = lax.broadcasted_iota(jnp.int32, shape, 0)
    time = lax.broadcasted_iota(jnp.int32, shape, 1) + my_wide * times
    order_copy.wait()
    order = jnp.zeros(shape, jnp.int32)
    for i in range(total):
        order = jnp.where(row >> 1 == i, orders[i], order)
    steps = order * time
    imag_row = (row & 1) == 1
    factor = 1.0 / math.sqrt(TIME)
    stacks, highs = [], []
    for shift in (jnp.where(imag_row, QUARTER, 0), jnp.where(imag_row, 0, 3 * QUARTER)):
        high, low = high_low(cosine(steps + shift) * factor)
        stacks.append(jnp.concatenate([high, low], axis=0))
        highs.append(high)

    for f in range(blocks):
        vis_copies[f].wait()
        both = jnp.zeros((4 * total, modes), jnp.float32)
        small = jnp.zeros((2 * total, modes), jnp.float32)
        for c in range(2):
            high, low = high_low(vis[c, f])
            both += lax.dot_general(stacks[c], high, NT, preferred_element_type=jnp.float32)
            small += lax.dot_general(highs[c], low, NT, preferred_element_type=jnp.float32)
        result = both[: 2 * total] + (both[2 * total :] + small)
        for w in range(wide):
            part[w, f] = result[rows * w : rows * (w + 1)]

    pl.semaphore_wait(barrier, len(greeted))
    sends = []
    for j in range(1, wide):
        target = lax.rem(my_wide + j, wide)
        copy = pltpu.make_async_remote_copy(
            src_ref=part.at[target],
            dst_ref=recv.at[j - 1],
            send_sem=send_sem.at[j - 1],
            recv_sem=recv_sem.at[j - 1],
            device_id={"wide": target},
            device_id_type=MESH,
        )
        copy.start()
        sends.append(copy)
    for copy in sends:
        copy.wait_recv()

    order_of_row = lax.broadcasted_iota(jnp.int32, (rows, modes), 0) >> 1
    targets = [{"freq": before}, {"freq": before, "pol": 1 - my_pol}, {"pol": 1 - my_pol}]
    proj_sends = []
    for f in range(blocks):
        summed = part[my_wide, f]
        for j in range(wide - 1):
            summed += recv[j, f]
        for o in range(local):
            ms_ref[o, f] = summed[2 * o : 2 * o + 2]
        other = turned(summed, 1)
        beam_copies[f].wait()
        acc = jnp.zeros((rows, beams.shape[-1]), jnp.float32)
        for o in range(local):
            mine = order_of_row == o
            for c, data in ((0, summed), (1, other)):
                left = jnp.where(mine, data, 0.0).astype(jnp.bfloat16)
                acc += lax.dot_general(
                    left, beams[o, f, c], NN, preferred_element_type=jnp.float32
                )
        proj[f] = acc
        for s, target in enumerate(targets):
            copy = pltpu.make_async_remote_copy(
                src_ref=proj.at[f],
                dst_ref=recv_proj.at[s, f],
                send_sem=psend_sem.at[s, f],
                recv_sem=precv_sem.at[s, f],
                device_id=target,
                device_id_type=MESH,
            )
            copy.start()
            proj_sends.append(copy)
    spectra_copy.wait()
    extended = []
    for f in range(blocks):
        proj_sends[3 * f + 2].wait_recv()
        extended.append(proj[f] + recv_proj[2, f])
    order_of_row = lax.broadcasted_iota(jnp.int32, (rows, beams.shape[-1]), 0) >> 1
    for f in range(blocks):
        if f in (0, blocks - 1):
            arriving = range(blocks - 1) if f == 0 else range(blocks - 1, blocks)
            for g in arriving:
                proj_sends[3 * g].wait_recv()
                proj_sends[3 * g + 1].wait_recv()
            extended += [recv_proj[0, g] + recv_proj[1, g] for g in arriving]
        mixed = spectra[0, f : f + 1] * extended[f]
        for d in range(1, BAND + 1):
            mixed = mixed + spectra[d, f : f + 1] * extended[f + d]
        other = turned(mixed, -1)
        acc = jnp.zeros((rows, modes), jnp.float32)
        for o in range(local):
            mine = order_of_row == o
            for c, data in ((0, mixed), (1, other)):
                left = jnp.where(mine, data, 0.0).astype(jnp.bfloat16)
                acc += lax.dot_general(
                    left, beams[o, f, c], NT, preferred_element_type=jnp.float32
                )
        for o in range(local):
            out_ref[o, f] = acc[2 * o : 2 * o + 2]
    for copy in sends + proj_sends:
        copy.wait_send()


def shards(wide, freq, visibilities, beams, spectra, m_orders):
    local, blocks, _, modes, degrees = beams.shape
    times = visibilities.shape[1]
    rows = 2 * local
    result = jax.ShapeDtypeStruct((2, local, blocks, 2, modes), jnp.float32)
    dma = pltpu.SemaphoreType.DMA
    both = pl.pallas_call(
        functools.partial(kernel, wide, freq),
        out_shape=result,
        in_specs=[pl.BlockSpec(memory_space=pl.ANY)] * 4,
        out_specs=pl.BlockSpec(memory_space=pltpu.VMEM),
        scratch_shapes=[
            pltpu.SMEM(m_orders.shape, jnp.int32),
            pltpu.VMEM((2, blocks, modes, times), jnp.float32),
            pltpu.VMEM(beams.shape, beams.dtype),
            pltpu.VMEM((BAND + 1, blocks, degrees), jnp.float32),
            pltpu.VMEM((wide, blocks, rows, modes), jnp.float32),
            pltpu.VMEM((wide - 1, blocks, rows, modes), jnp.float32),
            pltpu.VMEM((blocks, rows, degrees), jnp.float32),
            pltpu.VMEM((3, blocks, rows, degrees), jnp.float32),
            dma,
            dma((blocks,)),
            dma((blocks,)),
            dma,
            dma((wide - 1,)),
            dma((wide - 1,)),
            dma((3, blocks)),
            dma((3, blocks)),
        ],
        compiler_params=pltpu.CompilerParams(
            collective_id=0, has_side_effects=True, vmem_limit_bytes=48 << 20
        ),
    )(
        *(
            pltpu.with_memory_space_constraint(array, pltpu.HBM)
            for array in (
                m_orders,
                jnp.transpose(visibilities, (0, 2, 3, 1)),
                beams,
                jnp.transpose(spectra, (1, 0, 2)),
            )
        )
    )
    return both[0], both[1]


def solution(mesh):
    return jax.shard_map(
        functools.partial(shards, mesh.shape["wide"], mesh.shape["freq"]),
        mesh=mesh,
        in_specs=(
            P(None, ("grp", "wide"), "freq", "pol"),
            P("wide", "freq", None, "pol", None),
            P("freq", None, None),
            P(),
        ),
        out_specs=(
            P(("grp", "wide"), "freq", None, "pol"),
            P(("grp", "wide"), "freq", None, "pol"),
        ),
        check_vma=False,
    )
```
